128 devices in a mesh: dp: 8 (over z_hi, x), tensor: 16 (over y, z_lo, core).
Axes of the slice: x: 4, y: 4, z: 4 (z_hi: 2, z_lo: 2; z = z_hi * 2 + z_lo), core: 2. Of those that a mesh axis runs over, the one named last changes fastest.
Arguments:
- tokens: bfloat16 [8192, 3584], P(('dp', 'tensor')), may hold values from -6 to 6
- cotangent: bfloat16 [8192, 3584], P(('dp', 'tensor')), may hold values from -6 to 6
- gate_weight: bfloat16 [3584, 10240], P(None, 'tensor'), may hold values from -0.09375 to 0.09375
- up_weight: bfloat16 [3584, 10240], P(None, 'tensor'), may hold values from -0.09375 to 0.09375
- down_weight: bfloat16 [10240, 3584], P('tensor'), may hold values from -0.0625 to 0.0625
- adapter_first_factors: bfloat16 [3584, 128], replicated, may hold values from -0.09375 to 0.09375
- adapter_second_factors: bfloat16 [2, 64, 10240], P(None, None, 'tensor'), may hold values from -0.75 to 0.75
- down_factor_first: bfloat16 [64, 10240], P(None, 'tensor'), may hold values from -0.0625 to 0.0625
- down_factor_second: bfloat16 [64, 3584], replicated, may hold values from -0.75 to 0.75
Outputs:
- input_gradient: bfloat16 [8192, 3584], P(('dp', 'tensor'))
- adapter_first_gradient: float32 [3584, 128], replicated
- adapter_second_gradient: float32 [2, 64, 10240], P(None, None, 'tensor')
- down_first_gradient: float32 [64, 10240], P(None, 'tensor')
- down_second_gradient: float32 [64, 3584], replicated
The draws below stay inside these ranges and needn't reach their ends.
All inputs are finite; a program needn't handle non-finite values.
Results may differ from the reference program's by a relative error of at most 0.017.
Values may be sent and summed in bfloat16 or wider, within the bound.
No kernel may reach another device: no remote copies, remote signals or barrier semaphores. Data moves between devices by JAX's collectives and lax.ppermute only.
A program may use at most 128 MiB of HBM per device.

```python
import math
import jax
import jax.numpy as jnp
from jax import lax

MODEL_WIDTH = 3584
HIDDEN_UNITS = 10240
ADAPTER_RANK = 64
TOKEN_COUNT = 8192
N_TENSOR = 16


def levels(own_key, shape, pieces, low, high):
    loudness = 1.0
    for position, parts in pieces:
        draws = jax.random.uniform(jax.random.fold_in(jax.random.fold_in(own_key, 6), position), (parts,), jnp.float32, low / len(pieces), high / len(pieces))
        loudness = loudness * jnp.repeat(jnp.exp(draws), shape[position] // parts).reshape((-1,) + (1,) * (len(shape) - 1 - position))
    return loudness


def gaussian(rng, dims, spread, most, cuts=(), dtype=jnp.bfloat16):
    array = spread * jax.random.normal(rng, dims, jnp.float32)
    if cuts:
        array = array * levels(rng, dims, cuts, -0.22, 0.18)
    return jnp.clip(array, -most, most).astype(dtype)


def setup_inputs(seed: int = 0) -> dict:
    key_of = jax.random.split(jax.random.key(seed), 10)
    tokens = gaussian(key_of[0], (TOKEN_COUNT, MODEL_WIDTH), 1.0, 6.0, ((0, 128),))
    cotangent = gaussian(key_of[1], (TOKEN_COUNT, MODEL_WIDTH), 1.0, 6.0, ((0, 128),))
    gate_weight = gaussian(key_of[2], (MODEL_WIDTH, HIDDEN_UNITS), MODEL_WIDTH ** -0.5, 0.09375, ((1, 16),))
    up_weight = gaussian(key_of[3], (MODEL_WIDTH, HIDDEN_UNITS), MODEL_WIDTH ** -0.5, 0.09375, ((1, 16),))
    down_weight = gaussian(key_of[4], (HIDDEN_UNITS, MODEL_WIDTH), HIDDEN_UNITS ** -0.5, 0.0625, ((0, 16),))
    adapter_first_factors = gaussian(key_of[5], (MODEL_WIDTH, 2 * ADAPTER_RANK), MODEL_WIDTH ** -0.5, 0.09375)
    adapter_second_factors = gaussian(key_of[6], (2, ADAPTER_RANK, HIDDEN_UNITS), ADAPTER_RANK ** -0.5, 0.75, ((2, 16),))
    down_factor_first = gaussian(key_of[7], (ADAPTER_RANK, HIDDEN_UNITS), HIDDEN_UNITS ** -0.5, 0.0625, ((1, 16),))
    down_factor_second = gaussian(key_of[8], (ADAPTER_RANK, MODEL_WIDTH), ADAPTER_RANK ** -0.5, 0.75)
    return dict(tokens=tokens, cotangent=cotangent, gate_weight=gate_weight, up_weight=up_weight, down_weight=down_weight, adapter_first_factors=adapter_first_factors, adapter_second_factors=adapter_second_factors, down_factor_first=down_factor_first, down_factor_second=down_factor_second)


adapter_scale = 0.5

def contraction_rows(left, right):
    return lax.dot_general(left, right, (((0,), (0,)), ((), ())), preferred_element_type=jnp.float32)

def contract_columns(left, right):
    return lax.dot_general(left, right, (((1,), (1,)), ((), ())), preferred_element_type=jnp.float32)

def exact_rows(left, right):
    return lax.dot_general(left.astype(jnp.float32), right.astype(jnp.float32), (((0,), (0,)), ((), ())), precision=lax.Precision.HIGHEST, preferred_element_type=jnp.float32)

def exact_columns(left, right):
    return lax.dot_general(left.astype(jnp.float32), right.astype(jnp.float32), (((1,), (1,)), ((), ())), precision=lax.Precision.HIGHEST, preferred_element_type=jnp.float32)

def reference(tokens, cotangent, gate_weight, up_weight, down_weight, adapter_first_factors, adapter_second_factors, down_factor_first, down_factor_second):
    input_lowrank = jnp.dot(tokens, adapter_first_factors, preferred_element_type=jnp.float32).astype(jnp.bfloat16)
    gate_preactivation = jnp.dot(tokens, gate_weight, preferred_element_type=jnp.float32) + adapter_scale * jnp.dot(input_lowrank[:, :ADAPTER_RANK], adapter_second_factors[0], preferred_element_type=jnp.float32)
    up_preactivation = jnp.dot(tokens, up_weight, preferred_element_type=jnp.float32) + adapter_scale * jnp.dot(input_lowrank[:, ADAPTER_RANK:], adapter_second_factors[1], preferred_element_type=jnp.float32)
    sigmoid = jax.nn.sigmoid(gate_preactivation)
    active = gate_preactivation * sigmoid
    hidden = (active * up_preactivation).astype(jnp.bfloat16)
    hid_low = contract_columns(hidden, down_factor_first)
    output_gradient_lowrank = contract_columns(cotangent, down_factor_second).astype(jnp.bfloat16)
    hidden_gradient = contract_columns(cotangent, down_weight) + adapter_scale * jnp.dot(output_gradient_lowrank, down_factor_first, preferred_element_type=jnp.float32)
    gate_gradient = (hidden_gradient * up_preactivation * sigmoid * (1.0 + gate_preactivation * (1.0 - sigmoid))).astype(jnp.bfloat16)
    up_gradient = (hidden_gradient * active).astype(jnp.bfloat16)
    lowrank_projected = jnp.concatenate([contract_columns(gate_gradient, adapter_second_factors[0]), contract_columns(up_gradient, adapter_second_factors[1])], axis=1)
    span_width = HIDDEN_UNITS // N_TENSOR

    def add_block(block, total):
        offset = (block * span_width).astype(jnp.int32)
        gate_part = lax.dynamic_slice_in_dim(gate_gradient, offset, span_width, 1)
        up_part = lax.dynamic_slice_in_dim(up_gradient, offset, span_width, 1)
        wg_part = lax.dynamic_slice_in_dim(gate_weight, offset, span_width, 1)
        wu_part = lax.dynamic_slice_in_dim(up_weight, offset, span_width, 1)
        term = contract_columns(gate_part, wg_part) + contract_columns(up_part, wu_part)
        rounded = lax.optimization_barrier(term.astype(jnp.bfloat16))
        return total + rounded.astype(jnp.float32)
    frozen_matrix = lax.fori_loop(0, N_TENSOR, add_block, jnp.zeros((tokens.shape[0], MODEL_WIDTH), jnp.float32))
    input_gradient = (frozen_matrix + adapter_scale * exact_columns(lowrank_projected, adapter_first_factors)).astype(jnp.bfloat16)
    factor_matrix = adapter_scale / math.sqrt(TOKEN_COUNT)
    adapter_first_gradient = factor_matrix * exact_rows(tokens, lowrank_projected)
    adapter_second_gradient = factor_matrix * jnp.stack([contraction_rows(input_lowrank[:, :ADAPTER_RANK], gate_gradient), contraction_rows(input_lowrank[:, ADAPTER_RANK:], up_gradient)])
    down_first_gradient = factor_matrix * contraction_rows(output_gradient_lowrank, hidden)
    down_second_gradient = factor_matrix * exact_rows(hid_low, cotangent)
    return (input_gradient, adapter_first_gradient, adapter_second_gradient, down_first_gradient, down_second_gradient)
```

```python
import math

import jax
import jax.numpy as jnp
from jax import lax
from jax.sharding import PartitionSpec as P


SCALE = 0.5
BF = jnp.bfloat16
F32 = jnp.float32


def dot(a, b, dims):
    return lax.dot_general(a, b, (dims, ((), ())), preferred_element_type=F32)


def along_tensor(a, target):
    return lax.ppermute(a, "tensor", [(t, target(t)) for t in range(16)])


def up_y(a):
    return along_tensor(a, lambda t: (t + 4) % 16)


def down_y(a):
    return along_tensor(a, lambda t: (t + 12) % 16)


def swap_z(a):
    return along_tensor(a, lambda t: t ^ 2)


def swap_core(a):
    return along_tensor(a, lambda t: t ^ 1)


def add(a, b):
    return (a.astype(F32) + b.astype(F32)).astype(BF)


def gather_near(a):
    return [a, up_y(a), down_y(a), swap_z(a)]


def gather_far(near):
    a, below, above, other = near
    half = a.shape[0] // 2
    two = jnp.concatenate([up_y(below[:half]), down_y(above[half:])])
    return [two, up_y(other), down_y(other), swap_z(two)]


def both_cores(parts):
    mine = jnp.concatenate(parts)
    return jnp.concatenate([mine, swap_core(mine)])


def sum_cores(part):
    half = part.shape[0] // 2
    return add(part[:half], swap_core(part[half:]))


def sum_dp(values):
    for bit in (1, 2, 4):
        pairs = [(g, g ^ bit) for g in range(8)]
        sent = [v.astype(BF) for v in values]
        got = [lax.ppermute(v, "dp", pairs) for v in sent]
        values = [v.astype(F32) + g.astype(F32) for v, g in zip(sent, got)]
    return values


def shards(tokens, cotangent, gate_w, up_w, down_w, first, second, down_first, down_second):
    rows, width = tokens.shape
    units = gate_w.shape[1]
    rank = second.shape[1]
    token_total = rows * lax.axis_size("dp") * lax.axis_size("tensor")
    factor = SCALE / math.sqrt(token_total)
    t = lax.axis_index("tensor")
    y, z, core = t // 4, (t // 2) % 2, t % 2

    weights = jnp.concatenate([gate_w, up_w, first], axis=1)
    zero = jnp.zeros_like(second[0])
    spread = jnp.concatenate(
        [jnp.concatenate([second[0], zero], 1), jnp.concatenate([zero, second[1]], 1)], 0
    )

    tok_near = gather_near(tokens)
    cot_near = gather_near(cotangent)
    tok_far = gather_far(tok_near)
    cot_far = gather_far(cot_near)

    def forward(x):
        pre = dot(x, weights, ((1,), (0,)))
        low = pre[:, 2 * units :].astype(BF)
        pre = pre[:, : 2 * units] + SCALE * dot(low, spread, ((1,), (0,)))
        gate, upper = pre[:, :units], pre[:, units:]
        sig = jax.nn.sigmoid(gate)
        act = gate * sig
        hidden = (act * upper).astype(BF)
        return low, hidden, act, upper * sig * (1.0 + gate * (1.0 - sig))

    def backward(c, state):
        low, hidden, act, slope = state
        dy_low = dot(c, down_second, ((1,), (1,))).astype(BF)
        d_hidden = dot(c, down_w, ((1,), (1,))) + SCALE * dot(dy_low, down_first, ((1,), (0,)))
        grads = jnp.concatenate(
            [(d_hidden * slope).astype(BF), (d_hidden * act).astype(BF)], axis=1
        )
        u_low = dot(grads, spread, ((1,), (1,)))
        hid_low = dot(hidden, down_first, ((1,), (1,)))
        full = jnp.concatenate([grads, (SCALE * u_low).astype(BF)], axis=1)
        part = dot(full, weights, ((1,), (1,))).astype(BF)
        part = jnp.concatenate([part, u_low.astype(BF), hid_low.astype(BF)], axis=1)
        d_second = dot(low, grads, ((0,), (0,)))
        d_first = dot(dy_low, hidden, ((0,), (0,)))
        return part, d_second, d_first

    x0 = both_cores(tok_near)
    s0 = forward(x0)
    x1 = both_cores(tok_far)
    s1 = forward(x1)
    c0 = both_cores(cot_near)
    part0, ds0, df0 = backward(c0, s0)
    c1 = both_cores(cot_far)
    part1, ds1, df1 = backward(c1, s1)

    late = sum_cores(part1)
    early = sum_cores(part0)
    own, below, above, other = [early[i * rows : (i + 1) * rows] for i in range(4)]
    two, below_o, above_o, two_o = [late[i * rows : (i + 1) * rows] for i in range(4)]
    half = rows // 2
    two = add(two, swap_z(two_o))
    other = (
        other.astype(F32) + down_y(below_o).astype(F32) + up_y(above_o).astype(F32)
    ).astype(BF)
    below = jnp.concatenate([add(below[:half], down_y(two[:half])), below[half:]])
    above = jnp.concatenate([above[:half], add(above[half:], up_y(two[half:]))])
    total = (
        own.astype(F32)
        + swap_z(other).astype(F32)
        + down_y(below).astype(F32)
        + up_y(above).astype(F32)
    )
    input_gradient = total[:, :width].astype(BF)

    d_second = ds0 + ds1
    d_second = jnp.stack([d_second[:rank, :units], d_second[rank:, units:]])
    d_first = df0 + df1

    low_near = gather_near(total[:, width:].astype(BF))
    lows = jnp.concatenate([both_cores(low_near), both_cores(gather_far(low_near))])
    group_tok = jnp.concatenate([x0, x1])
    group_cot = jnp.concatenate([c0, c1])
    span = width // 16
    tok_slice = lax.dynamic_slice_in_dim(group_tok, t * span, span, 1)
    cot_slice = lax.dynamic_slice_in_dim(group_cot, t * span, span, 1)
    mine = jnp.concatenate(
        [
            dot(tok_slice, lows[:, : 2 * rank], ((0,), (0,))),
            dot(cot_slice, lows[:, 2 * rank :], ((0,), (0,))),
        ],
        axis=1,
    )
    mine, d_second, d_first = sum_dp([mine, d_second, d_first])
    mine = (factor * mine).astype(BF)
    near = gather_near(mine)
    far = gather_far(near)
    own, below, above, other = near
    two, below_o, above_o, two_o = far
    chip = jnp.stack(
        [jnp.stack(p) for p in ((own, other), (above, above_o), (two, two_o), (below, below_o))]
    )
    chip = jnp.where(z == 0, chip, chip[:, ::-1])
    theirs = swap_core(chip)
    pair = jnp.where(core == 0, jnp.stack([chip, theirs], 2), jnp.stack([theirs, chip], 2))
    ring = jnp.concatenate([pair, pair])
    ordered = lax.dynamic_slice_in_dim(ring, (4 - y) % 4, 4, 0)
    ordered = ordered.reshape(width, 3 * rank).astype(F32)
    return (
        input_gradient,
        ordered[:, : 2 * rank],
        factor * d_second,
        factor * d_first,
        ordered[:, 2 * rank :].T,
    )


def solution(mesh):
    in_specs = (
        P(("dp", "tensor"), None),
        P(("dp", "tensor"), None),
        P(None, "tensor"),
        P(None, "tensor"),
        P("tensor", None),
        P(),
        P(None, None, "tensor"),
        P(None, "tensor"),
        P(),
    )
    out_specs = (P(("dp", "tensor"), None), P(), P(None, None, "tensor"), P(None, "tensor"), P())
    return jax.shard_map(shards, mesh=mesh, in_specs=in_specs, out_specs=out_specs, check_vma=False)
```
